256 devices in a mesh: dp: 8 (over x, core), expert: 32 (over y, z).
Axes of the slice: x: 4, y: 4, z: 8, core: 2. Of those that a mesh axis runs over, the one named last changes fastest.
Arguments:
- tokens: bfloat16 [8, 4096, 4096], P('dp', 'expert'), may hold values from -6 to 6
- norm_gain: float32 [4096], replicated, may hold values from 0.5 to 1.5
- router_weight: float32 [32, 4096], replicated, may hold values from -0.09375 to 0.09375
- value_weight: float32 [4096], replicated, may hold values from -0.09375 to 0.09375
- gate_weight: bfloat16 [32, 1536, 4096], P('expert', 'dp'), may hold values from -0.09375 to 0.09375
- up_weight: bfloat16 [32, 1536, 4096], P('expert', 'dp'), may hold values from -0.09375 to 0.09375
- down_weight: bfloat16 [32, 1536, 4096], P('expert', 'dp'), may hold values from -0.15625 to 0.15625
- routes: int32 [8, 4096, 2], P('dp', 'expert'), may hold values from 0 to 31, all different within a row; in each aligned block of 128 rows (0 to 127, 128 to 255, ..., all dimensions but the last counted through in order) at most 12 rows name the same one
- segment_ids: int32 [8, 4096], P('dp', 'expert'), may hold values from 0 to 7, never falling along the last dimension, each value on 1 to 1024 neighbouring positions
- loss_mask: int32 [8, 4096], P('dp', 'expert'), may hold values 0 or 1
- penalty_reward: float32 [8, 4096], P('dp', 'expert'), may hold values from -0.3 to 0.3
- scores: float32 [8, 8], P('dp'), may hold values from -6 to 6
Outputs:
- values: float32 [8, 4096], P('dp', 'expert')
- mean_loss: float32 [], replicated
- value_grad: float32 [4096], replicated
- router_grad: float32 [32, 4096], replicated
- gate_grad: bfloat16 [32, 1536, 4096], P('expert', 'dp')
- up_grad: bfloat16 [32, 1536, 4096], P('expert', 'dp')
- down_grad: bfloat16 [32, 1536, 4096], P('expert', 'dp')
The draws below stay inside these ranges and needn't reach their ends.
Inputs may be any that keep to these rules, and one draw needn't show every extreme that they name: Each token names 2 different experts; within the tokens of one device no expert is named by more than 12 routes, a bound that some block reaches. `segment_ids`: within each data row the ids never fall; each response holds 1 to 1024 tokens and one holds exactly 1024.
All inputs are finite; a program needn't handle non-finite values. No bound on the sum of `loss_mask` on one device may be relied on, other than what follows from the above.
Results may differ from the reference program's by a relative error of at most 0.0069.
Values may be sent and summed in bfloat16 or wider, within the bound.
No kernel may reach another device: no remote copies, remote signals or barrier semaphores. Data moves between devices by JAX's collectives and lax.ppermute only.
A program may use at most 192 MiB of HBM per device.

```python
import functools
import math
import jax
import jax.numpy as jnp
import numpy as np
from jax import lax

D = 4096
FF = 1536
TOPK = 2
SEGS = 8
TOK_DEV = 128
EXPERTS = 32
ROW_TOK = 4096
MOST = 1024
CAP = 12
N_DP = 8
N_EXPERT = 32


def plant(array, stream_key, low, top_value):
    place = [jax.random.randint(jax.random.fold_in(stream_key, axis), (), 0, length) for axis, length in enumerate(array.shape)]
    widest = array.shape.index(max(array.shape))
    next_to = place[:widest] + [(place[widest] + 1) % array.shape[widest]] + place[widest + 1:]
    return array.at[tuple(place)].set(low).at[tuple(next_to)].set(top_value)


def shard_levels(key, shape, split, least, high):
    gain, own = 1.0, jax.random.fold_in(key, 6)
    for axis_at, shards_of in split:
        draws = jnp.exp(jax.random.uniform(jax.random.fold_in(own, axis_at), (shards_of,), jnp.float32, least / len(split), high / len(split)))
        gain = gain * jnp.repeat(draws, shape[axis_at] // shards_of).reshape([-1 if axis == axis_at else 1 for axis in range(len(shape))])
    return gain


def split_up(number_of, total, bound, slope):
    loads = [(1 << 20) // math.isqrt(standing ** slope) + 1 for standing in range(2, number_of + 1)]
    rest, given = total - bound - (number_of - 1), [1] * (number_of - 1)
    while rest > 0:
        candidates = [i for i in range(number_of - 1) if given[i] < bound]
        pool, left = sum([loads[i] for i in candidates]), rest
        for i in candidates:
            extra = min(bound - given[i], max(1, left * loads[i] // pool), rest)
            given[i] = given[i] + extra
            rest = rest - extra
    return np.array([bound] + given)


def ragged(rng, count, total, bound, slope):
    if count == 2:
        one = jax.random.randint(rng, (), max(1, total - bound), min(bound, total - 1) + 1)
        return jnp.stack([one, total - one])
    sizes = jnp.asarray(split_up(count, total, bound, slope), jnp.int32)
    twos = (count - 1) // 2
    giver, receiver = sizes[1:1 + 2 * twos:2], sizes[2:2 + 2 * twos:2]
    room = jnp.minimum(giver - 1, bound - receiver)
    shifted = jax.random.randint(jax.random.fold_in(rng, 1), (twos,), 0, 1 << 20) % (room + 1)
    sizes = sizes.at[1:1 + 2 * twos:2].set(giver - shifted).at[2:2 + 2 * twos:2].set(receiver + shifted)
    return sizes[jax.random.permutation(jax.random.fold_in(rng, 2), count)]


def shared_out(key, own, number, rows, amount, top, reach, slope):
    ranking = jax.random.permutation(key, amount)
    packed, ordinary = load_shares(amount, rows * top, reach, slope, True), load_shares(amount, rows * top, reach, slope, False)
    places = jnp.arange(amount)

    def named(lengths, rotation):
        used = int((lengths > 0).sum())
        fixed = max(1, used // 4)
        passed = fixed + (places - fixed + rotation * (used - fixed)) % max(1, amount - fixed)
        return jnp.zeros((amount,), jnp.int32).at[ranking[jnp.where(places < fixed, places, passed)]].set(jnp.asarray(lengths, jnp.int32))

    lengths = jnp.where(number % 4 == 0, named(packed, number // 4), named(ordinary, number - number // 4 - 1))
    mixed = jax.random.permutation(jax.random.fold_in(own, 3), amount)
    giver, receiver = mixed[0:amount // 2 * 2:2], mixed[1:amount // 2 * 2:2]
    room = jnp.minimum(lengths[giver] - 1, reach - lengths[receiver]) // 2
    room = jnp.where((giver == ranking[0]) | (receiver == ranking[0]) | (lengths[receiver] == 0), 0, jnp.maximum(room, 0))
    passed = jax.random.randint(jax.random.fold_in(own, 4), (amount // 2,), 0, 1 << 20) % (room + 1)
    lengths = lengths.at[giver].add(-passed).at[receiver].add(passed)
    members = jnp.searchsorted(jnp.cumsum(lengths), jnp.arange(rows * top), side="right").astype(jnp.int32)
    grid = members.reshape(top, rows).T
    grid = grid[jax.random.permutation(jax.random.fold_in(own, 1), rows)]
    rotation = jax.random.randint(jax.random.fold_in(own, 2), (rows, 1), 0, top)
    return jnp.take_along_axis(grid, (jnp.arange(top)[None, :] + rotation) % top, axis=1)


def load_shares(count, total, reach, skew, full):
    loads = [(1 << 20) // math.isqrt(grade ** skew) + 1 for grade in range(1, count + 1)]
    largest = reach if full else min(reach, max(-(-total // count), total * loads[0] // sum(loads)))
    least = 1 if total - largest >= count - 1 else 0
    holding, surplus = [largest] + [least] * (count - 1), total - largest - least * (count - 1)
    while surplus > 0:
        movable = [i for i in range(1, count) if holding[i] < largest] or [i for i in range(1, count) if holding[i] < reach]
        whole, left = sum([loads[i] for i in movable]), surplus
        for i in movable:
            addition = min(reach - holding[i], max(1, left * loads[i] // whole), surplus)
            holding[i] = holding[i] + addition
            surplus = surplus - addition
    return np.array(holding)


def noise(key, shape, width, limit, split=(), kind=jnp.bfloat16):
    array = width * jax.random.normal(key, shape, jnp.float32)
    if split:
        array = array * shard_levels(key, shape, split, -0.22, 0.18)
    return jnp.clip(array, -limit, limit).astype(kind)


def setup_inputs(seed: int = 0) -> dict:
    arg_keys = jax.random.split(jax.random.key(seed), 13)
    tokens = noise(arg_keys[0], (N_DP, ROW_TOK, D), 1.0, 6.0, ((0, 8), (1, 32)))
    norm_gain = jnp.clip(1.0 + 0.1 * jax.random.normal(arg_keys[1], (D,), jnp.float32), 0.5, 1.5)
    router_weight = noise(arg_keys[2], (EXPERTS, D), D ** -0.5, 0.09375, (), jnp.float32)
    value_weight = noise(arg_keys[3], (D,), D ** -0.5, 0.09375, (), jnp.float32)
    gate_weight = noise(arg_keys[4], (EXPERTS, FF, D), D ** -0.5, 0.09375, ((0, 32), (1, 8)))
    up_weight = noise(arg_keys[5], (EXPERTS, FF, D), D ** -0.5, 0.09375, ((0, 32), (1, 8)))
    down_weight = noise(arg_keys[6], (EXPERTS, FF, D), FF ** -0.5, 0.15625, ((0, 32), (1, 8)))
    routes_keys = jax.random.split(jax.random.fold_in(arg_keys[7], 1), N_DP * ROW_TOK // TOK_DEV)
    routes_turns = jax.random.permutation(jax.random.fold_in(arg_keys[7], 3), N_DP * ROW_TOK // TOK_DEV)
    routes = jax.vmap(lambda own, number: shared_out(jax.random.fold_in(arg_keys[7], 2), own, number, TOK_DEV, EXPERTS, TOPK, CAP, 2))(routes_keys, routes_turns).reshape((N_DP, ROW_TOK, TOPK))
    segment_ids = jax.vmap(lambda own: jnp.searchsorted(jnp.cumsum(ragged(own, SEGS, ROW_TOK, MOST, 1)), jnp.arange(ROW_TOK), side="right"))(jax.random.split(arg_keys[8], N_DP)).reshape((N_DP, ROW_TOK)).astype(jnp.int32)
    loss_mask = plant((jax.random.randint(arg_keys[9], (N_DP, ROW_TOK), 0, 4) < 3).astype(jnp.int32), jax.random.fold_in(arg_keys[9], 1), 0, 1)
    penalty_reward = noise(arg_keys[10], (N_DP, ROW_TOK), 0.05, 0.3, ((0, 8), (1, 32)), jnp.float32)
    scores = noise(arg_keys[11], (N_DP, SEGS), 1.0, 6.0, ((0, 8),), jnp.float32)
    return dict(tokens=tokens, norm_gain=norm_gain, router_weight=router_weight, value_weight=value_weight, gate_weight=gate_weight, up_weight=up_weight, down_weight=down_weight, routes=routes, segment_ids=segment_ids, loss_mask=loss_mask, penalty_reward=penalty_reward, scores=scores)


discount_rate = 0.9995
norm_epsilon = 1e-06
white_epsilon = 1e-05
highest = lax.Precision.HIGHEST

def norm_rows(tokens, norm_gain):
    as_float = tokens.astype(jnp.float32)
    inverse_rms = lax.rsqrt(lax.optimization_barrier(jnp.mean(as_float * as_float, axis=-1, keepdims=True)) + norm_epsilon)
    return (as_float * inverse_rms * norm_gain).astype(jnp.bfloat16)

def slot_numbers(block_routes, experts):
    flattened = block_routes.reshape(-1)
    onehot = (flattened[:, None] == jnp.arange(experts, dtype=jnp.int32)[None, :]).astype(jnp.int32)
    before = jnp.cumsum(onehot, axis=0) - onehot
    return lax.optimization_barrier(jnp.sum(before * onehot, axis=1)).astype(jnp.int32).reshape(block_routes.shape)

def row_returns(reward, segment):
    following = jnp.concatenate([segment[1:], jnp.full((1,), -1, jnp.int32)])
    same_next = (following == segment).astype(jnp.float32)

    def backward_step(carry, item):
        reward_now, same = item
        result = reward_now + discount_rate * carry * same
        return (result, result)
    final_carry, result = lax.scan(backward_step, jnp.zeros((), jnp.float32), (reward, same_next), reverse=True)
    return result

def reference(tokens, norm_gain, router_weight, value_weight, gate_weight, up_weight, down_weight, routes, segment_ids, loss_mask, penalty_reward, scores):
    blocks = N_DP * N_EXPERT
    all_tokens = blocks * TOK_DEV
    flat_tokens = tokens.reshape(all_tokens, D)
    normed = norm_rows(flat_tokens, norm_gain)
    flat_routes = routes.reshape(all_tokens, TOPK)
    last_last = (((1,), (1,)), ((), ()))
    first_first = (((0,), (0,)), ((), ()))
    logits = lax.dot_general(normed.astype(jnp.float32), router_weight, last_last, precision=highest)
    chosen = jnp.take_along_axis(logits, flat_routes, axis=1)
    gate_sigmoid = jax.nn.sigmoid(chosen)
    sigmoid_total = lax.optimization_barrier(jnp.sum(gate_sigmoid, axis=1, keepdims=True))
    route_prob = gate_sigmoid / sigmoid_total
    slot_number = jax.vmap(functools.partial(slot_numbers, experts=EXPERTS))(flat_routes.reshape(blocks, TOK_DEV, TOPK)).reshape(all_tokens, TOPK)
    block_of = jnp.arange(all_tokens, dtype=jnp.int32) // TOK_DEV
    token_ids = jnp.broadcast_to(jnp.arange(all_tokens, dtype=jnp.int32)[:, None], (all_tokens, TOPK))
    slot_place = ((flat_routes * blocks + block_of[:, None]) * CAP + slot_number).reshape(-1)
    source_index = jnp.full((EXPERTS * blocks * CAP,), all_tokens, jnp.int32).at[slot_place].set(token_ids.reshape(-1))
    source_index = source_index.reshape(EXPERTS, blocks * CAP)
    padded = jnp.concatenate([normed, jnp.zeros((1, D), jnp.bfloat16)], axis=0)

    def forward_one(inputs):
        index_row, gate_mat, up_mat, down_mat = inputs
        expert_rows = padded[index_row]
        gate_value = lax.dot_general(expert_rows, gate_mat, last_last, preferred_element_type=jnp.float32)
        up_value = lax.dot_general(expert_rows, up_mat, last_last, preferred_element_type=jnp.float32)
        hidden = (gate_value * jax.nn.sigmoid(gate_value) * up_value).astype(jnp.bfloat16)
        value_along = jnp.dot(down_mat.astype(jnp.float32), value_weight, precision=highest)
        return (jnp.dot(hidden.astype(jnp.float32), value_along, precision=highest), gate_value, up_value)
    row_values, gate_all, up_all = lax.map(forward_one, (source_index, gate_weight, up_weight, down_weight))
    route_value = row_values.reshape(-1)[slot_place].reshape(all_tokens, TOPK)
    flat_values = jnp.dot(flat_tokens.astype(jnp.float32), value_weight, precision=highest) + lax.optimization_barrier(jnp.sum(route_prob * route_value, axis=1))
    values = flat_values.reshape(N_DP, ROW_TOK)
    following = jnp.concatenate([segment_ids[:, 1:], jnp.full((N_DP, 1), -1, jnp.int32)], axis=1)
    ending = following != segment_ids
    segment_hit = segment_ids[:, :, None] == jnp.arange(SEGS, dtype=jnp.int32)[None, None, :]
    score_pick = lax.optimization_barrier(jnp.sum(jnp.where(segment_hit, scores[:, None, :], 0.0), axis=2))
    reward = penalty_reward + jnp.where(ending, score_pick, 0.0)
    returns = jax.vmap(row_returns)(reward, segment_ids)
    mask_float = loss_mask.astype(jnp.float32)
    divisor = jnp.maximum(jnp.sum(mask_float), 1.0)
    centre = jnp.sum(mask_float * returns) / divisor
    variance = jnp.sum(mask_float * (returns - centre) * (returns - centre)) / divisor
    whitened = (returns - centre) * lax.rsqrt(variance + white_epsilon)
    value_error = mask_float * (values - whitened)
    mean_loss = 0.5 * jnp.sum(mask_float * (values - whitened) * (values - whitened)) / divisor
    flat_error = value_error.reshape(all_tokens)
    route_weight = flat_error[:, None] * route_prob
    prob_grad = flat_error[:, None] * route_value
    weight_table = jnp.zeros((EXPERTS * blocks * CAP,), jnp.float32).at[slot_place].set(route_weight.reshape(-1))
    weight_table = weight_table.reshape(EXPERTS, blocks * CAP)

    def backward_one(inputs):
        index_row, row_weight, gate_value, up_value, down_mat = inputs
        expert_rows = padded[index_row]
        gate_sig = jax.nn.sigmoid(gate_value)
        hidden = (gate_value * gate_sig * up_value).astype(jnp.bfloat16)
        down_float = down_mat.astype(jnp.float32)
        value_along = jnp.dot(down_float, value_weight, precision=highest)
        spread = jnp.dot(row_weight, hidden.astype(jnp.float32), precision=highest)
        down_part = (spread[:, None] * value_weight[None, :]).astype(jnp.bfloat16)
        hidden_grad = row_weight[:, None] * value_along[None, :]
        gate_delta = (hidden_grad * up_value * gate_sig * (1.0 + gate_value * (1.0 - gate_sig))).astype(jnp.bfloat16)
        up_delta = (hidden_grad * gate_value * gate_sig).astype(jnp.bfloat16)
        gate_part = lax.dot_general(gate_delta, expert_rows, first_first, preferred_element_type=jnp.float32).astype(jnp.bfloat16)
        up_part = lax.dot_general(up_delta, expert_rows, first_first, preferred_element_type=jnp.float32).astype(jnp.bfloat16)
        head_part = jnp.dot(spread, down_float, precision=highest)
        return (gate_part, up_part, down_part, head_part)
    gate_grad, up_grad, down_grad, head_parts = lax.map(backward_one, (source_index, weight_table, gate_all, up_all, down_weight))
    value_grad = jnp.dot(flat_error, flat_tokens.astype(jnp.float32), precision=highest) + lax.optimization_barrier(jnp.sum(head_parts, axis=0))
    sigma_grad = (prob_grad - lax.optimization_barrier(jnp.sum(prob_grad * route_prob, axis=1, keepdims=True))) / sigmoid_total
    chosen_grad = sigma_grad * gate_sigmoid * (1.0 - gate_sigmoid)
    expert_hit = flat_routes[:, :, None] == jnp.arange(EXPERTS, dtype=jnp.int32)[None, None, :]
    logit_grad = lax.optimization_barrier(jnp.sum(jnp.where(expert_hit, chosen_grad[:, :, None], 0.0), axis=1))
    router_grad = lax.dot_general(logit_grad, normed.astype(jnp.float32), first_first, precision=highest)
    return (values, mean_loss, value_grad, router_grad, gate_grad, up_grad, down_grad)
```

```python
import functools

import functools

import jax
import jax.numpy as jnp
from jax import lax
from jax.experimental import pallas as pl
from jax.experimental.pallas import tpu as pltpu
from jax.sharding import PartitionSpec as P


discount_rate = 0.9995
norm_epsilon = 1e-06
white_epsilon = 1e-05
highest = lax.Precision.HIGHEST
chunks = 3
stat_lane = 64
last_last = (((1,), (1,)), ((), ()))
plain = (((1,), (0,)), ((), ()))


def passed_along(array, axis, by):
    size = lax.axis_size(axis)
    pairs = [(i, i + by) for i in range(size) if 0 <= i + by < size]
    return lax.ppermute(array, axis, pairs)


def to_all(array, axis):
    size = lax.axis_size(axis)
    return lax.all_to_all(
        jnp.broadcast_to(array[None], (size,) + array.shape), axis, 0, 0, tiled=True
    )


def norm_rows(tokens, norm_gain):
    as_float = tokens.astype(jnp.float32)
    inverse_rms = lax.rsqrt(jnp.mean(as_float * as_float, axis=-1, keepdims=True) + norm_epsilon)
    return (as_float * inverse_rms * norm_gain).astype(jnp.bfloat16)


def ring(block, dp_count):
    half = block.shape[0] // 2
    up = [(i, (i + 2) % dp_count) for i in range(dp_count)]
    down = [(i, (i - 2) % dp_count) for i in range(dp_count)]
    other = [(i, i ^ 1) for i in range(dp_count)]
    below = lax.ppermute(block, "dp", up)
    above = lax.ppermute(block, "dp", down)
    far_first = lax.ppermute(below[:half], "dp", up)
    far_second = lax.ppermute(above[half:], "dp", down)
    near, far = [block, below, above], [far_first, far_second]
    near_twins = [lax.ppermute(piece, "dp", other) for piece in near]
    far_twins = [lax.ppermute(piece, "dp", other) for piece in far]
    return near + near_twins, far + far_twins


def relative_blocks(dp_count):
    place = lax.axis_index("dp")
    chip, core = place // 2, place % 2
    chips = dp_count // 2
    places = [(twin, shift) for twin in (0, 1) for shift in (0, chips - 1, 1)] + [(0, 2), (1, 2)]
    return [((chip + shift) % chips) * 2 + (core ^ twin) for twin, shift in places]


def first_kernel(seg_ref, mask_ref, pen_ref, score_ref, mark_ref, own_ref, local_ref, reach_ref):
    tok = seg_ref.shape[1]
    segment = seg_ref[...].astype(jnp.float32)
    last = segment[:, tok - 1 :]
    carries = (mark_ref[...].astype(jnp.float32) == last + 1.0).astype(jnp.float32)
    lane = lax.broadcasted_iota(jnp.int32, (1, tok), 1).astype(jnp.float32)
    side = jnp.transpose(jnp.broadcast_to(segment, (tok, tok)))
    at_row = lax.broadcasted_iota(jnp.int32, (tok, tok), 0).astype(jnp.float32)
    at_lane = lax.broadcasted_iota(jnp.int32, (tok, tok), 1).astype(jnp.float32)
    same = side == jnp.broadcast_to(segment, (tok, tok))
    next_same = jnp.sum(
        jnp.where(same & (at_row == at_lane + 1.0), 1.0, 0.0), axis=0, keepdims=True
    )
    next_same = jnp.where(lane == tok - 1.0, carries, next_same)
    picked = jnp.zeros((1, tok), jnp.float32)
    for which in range(score_ref.shape[1]):
        picked = picked + jnp.where(
            segment == float(which), score_ref[:, which : which + 1], 0.0
        )
    reward = pen_ref[...] + jnp.where(next_same == 0.0, picked, 0.0)
    log_rate = jnp.log(jnp.float32(discount_rate))
    rewards = jnp.transpose(jnp.broadcast_to(reward, (tok, tok)))
    ahead = at_row - at_lane
    local = jnp.sum(
        jnp.where(same & (ahead >= 0.0), jnp.exp(ahead * log_rate) * rewards, 0.0),
        axis=0,
        keepdims=True,
    )
    reach = jnp.where(segment == last, jnp.exp((tok - lane) * log_rate), 0.0) * carries
    mask = mask_ref[...].astype(jnp.float32)
    count = jnp.sum(mask, axis=1, keepdims=True)
    safe = jnp.maximum(count, 1.0)
    mean_local = jnp.sum(mask * local, axis=1, keepdims=True) / safe
    mean_reach = jnp.sum(mask * reach, axis=1, keepdims=True) / safe
    off_local = local - mean_local
    off_reach = reach - mean_reach
    parts = [
        reach[:, :1],
        local[:, :1],
        count,
        mean_local,
        mean_reach,
        jnp.sum(mask * off_local * off_local, axis=1, keepdims=True),
        jnp.sum(mask * off_local * off_reach, axis=1, keepdims=True),
        jnp.sum(mask * off_reach * off_reach, axis=1, keepdims=True),
    ]
    own = jnp.zeros((1, 128), jnp.float32)
    spot = lax.broadcasted_iota(jnp.int32, (1, 128), 1)
    for at, part in enumerate(parts):
        own = jnp.where(spot == stat_lane + at, part, own)
    own_ref[...] = own
    local_ref[...] = local
    reach_ref[...] = reach


def whiten(everyone, stride, place, local, reach):
    size = everyone.shape[0]
    table = jnp.transpose(everyone)[stat_lane : stat_lane + 8]
    lane = lax.broadcasted_iota(jnp.int32, (1, size), 1)
    factor, term = table[0:1], table[1:2]
    step = stride
    while step < size:
        inside = lane + step < size
        next_factor = jnp.where(inside, pltpu.roll(factor, size - step, 1), 1.0)
        next_term = jnp.where(inside, pltpu.roll(term, size - step, 1), 0.0)
        term = term + factor * next_term
        factor = factor * next_factor
        step *= 2
    carry = jnp.where(lane + stride < size, pltpu.roll(term, size - stride, 1), 0.0)
    counts = table[2:3]
    means = table[3:4] + table[4:5] * carry
    squares = table[5:6] + 2.0 * carry * table[6:7] + carry * carry * table[7:8]
    total = jnp.sum(counts, axis=1, keepdims=True)
    divisor = jnp.maximum(total, 1.0)
    centre = jnp.sum(counts * means, axis=1, keepdims=True) / divisor
    apart = means - centre
    square = jnp.sum(squares + counts * apart * apart, axis=1, keepdims=True)
    here = jnp.sum(jnp.where(lane == place, carry, 0.0), axis=1, keepdims=True)
    returns = local + reach * here
    return (returns - centre) * lax.rsqrt(square / divisor + white_epsilon), divisor


def forward_kernel(count, chained, offset, *refs):
    pieces = refs[:count]
    gate_ref, up_ref, along_ref = refs[count : count + 3]
    refs = refs[count + 3 + chained :]
    rows_ref, gates_ref, ups_ref, hidden_ref, part_ref, held, into, out = refs
    copies = []
    start = 0
    for at, piece in enumerate(pieces):
        span = piece.shape[0]
        copy = pltpu.make_async_copy(piece, held.at[pl.ds(start, span)], into.at[at])
        copy.start()
        copies.append(copy)
        start += span
    for copy in copies:
        copy.wait()
    back = pltpu.make_async_copy(held, rows_ref.at[pl.ds(offset, start)], out)
    back.start()
    pair = 256

    @pl.loop(0, start // pair)
    def _(turn):
        at = pl.multiple_of(turn * pair, pair)
        rows = held[pl.ds(at, pair), :]
        gate = lax.dot_general(
            gate_ref[...], rows, last_last, preferred_element_type=jnp.float32
        )
        up = lax.dot_general(up_ref[...], rows, last_last, preferred_element_type=jnp.float32)
        along = along_ref[...]
        sig = jax.nn.sigmoid(gate)
        swish = gate * sig
        hidden = (swish * up).astype(jnp.bfloat16)
        gates_ref[:, pl.ds(at, pair)] = along * up * sig * (1.0 + gate * (1.0 - sig))
        ups_ref[:, pl.ds(at, pair)] = along * swish
        hidden_ref[:, pl.ds(at, pair)] = hidden
        part_ref[:, pl.ds(at, pair)] = jnp.sum(
            hidden.astype(jnp.float32) * along, axis=0, keepdims=True
        )

    back.wait()


def forward(pieces, gate, up, along, rows, offset, all_rows):
    total = sum(piece.shape[0] for piece in pieces)
    width = pieces[0].shape[1]
    hidden = gate.shape[0]
    count = len(pieces)
    vmem = pl.BlockSpec(memory_space=pltpu.VMEM)
    far = pl.BlockSpec(memory_space=pl.ANY)
    chained = [] if rows is None else [rows]
    return pl.pallas_call(
        functools.partial(forward_kernel, count, len(chained), offset),
        out_shape=(
            jax.ShapeDtypeStruct((all_rows, width), jnp.bfloat16),
            jax.ShapeDtypeStruct((hidden, total), jnp.float32),
            jax.ShapeDtypeStruct((hidden, total), jnp.float32),
            jax.ShapeDtypeStruct((hidden, total), jnp.bfloat16),
            jax.ShapeDtypeStruct((1, total), jnp.float32),
        ),
        in_specs=[far] * count + [vmem] * 3 + [far] * len(chained),
        out_specs=(far, vmem, vmem, vmem, vmem),
        input_output_aliases={count + 3: 0} if chained else {},
        scratch_shapes=[
            pltpu.VMEM((total, width), jnp.bfloat16),
            pltpu.SemaphoreType.DMA((count,)),
            pltpu.SemaphoreType.DMA,
        ],
        compiler_params=pltpu.CompilerParams(vmem_limit_bytes=40 << 20),
        cost_estimate=pl.CostEstimate(
            flops=4 * total * width * hidden,
            bytes_accessed=4 * total * width + 4 * hidden * width,
            transcendentals=0,
        ),
    )(*pieces, gate, up, along, *chained)


def grad_kernel(chained, delta_ref, rows_ref, *refs):
    gate_ref, up_ref = refs[chained:]
    hidden = gate_ref.shape[0]
    both = lax.dot_general(
        delta_ref[...], rows_ref[...], plain, preferred_element_type=jnp.float32
    ).astype(jnp.bfloat16)
    gate_ref[...] = both[:hidden]
    up_ref[...] = both[hidden:]


def grads(delta, rows, tile, first, count, made):
    total, width = rows.shape
    hidden = delta.shape[0] // 2
    far = pl.BlockSpec(memory_space=pl.ANY)
    out = pl.BlockSpec((hidden, tile), lambda at: (0, at + first))
    return pl.pallas_call(
        functools.partial(grad_kernel, len(made)),
        grid=(count,),
        out_shape=(jax.ShapeDtypeStruct((hidden, width), jnp.bfloat16),) * 2,
        in_specs=[
            pl.BlockSpec(delta.shape, lambda at: (0, 0)),
            pl.BlockSpec((total, tile), lambda at: (0, at + first)),
        ]
        + [far] * len(made),
        out_specs=(out, out),
        input_output_aliases={2: 0, 3: 1} if made else {},
        compiler_params=pltpu.CompilerParams(vmem_limit_bytes=40 << 20),
        cost_estimate=pl.CostEstimate(
            flops=4 * total * hidden * tile * count,
            bytes_accessed=2 * total * tile * count,
            transcendentals=0,
        ),
    )(delta, rows, *made)


def pack_kernel(expert_count, slots, turns, block_ref, *refs):
    parts, own_ref, out_ref = refs[:-2], refs[-2], refs[-1]
    own = jnp.broadcast_to(own_ref[...], (8, own_ref.shape[1]))
    lanes = expert_count * slots
    row = lax.broadcasted_iota(jnp.int32, (8, lanes), 0)
    lane = lax.broadcasted_iota(jnp.int32, (8, lanes), 1)
    ordered = []
    for held in turns:
        total = jnp.zeros((8, lanes), jnp.float32)
        found = [(which, at) for which, many in held for at in range(many)]
        for at, (which, within) in enumerate(found):
            piece = parts[which][:, within * lanes : (within + 1) * lanes]
            total = jnp.where(row == block_ref[at], jnp.broadcast_to(piece, (8, lanes)), total)
        ordered.append(total)
    for expert in range(expert_count):
        message = own
        for at, part in enumerate(ordered):
            shift = (at * slots - expert * slots) % lanes
            moved = pltpu.roll(part, shift, 1) if shift else part
            message = jnp.where((lane >= at * slots) & (lane < (at + 1) * slots), moved, message)
        out_ref[expert] = message


def value_kernel(
    capacity, place_ref, got_ref, slot_ref, logit_ref, own_ref, local_ref, reach_ref, mask_ref,
    out_ref, val_ref, err_ref, loss_ref, div_ref
):
    experts, tok = slot_ref.shape
    slot = slot_ref[...]
    got = got_ref[...]
    returned = jnp.sum(got, axis=1)
    stride = got.shape[1]
    white, divisor = whiten(
        got.reshape(got.shape[0] * stride, got.shape[2]),
        stride,
        place_ref[0],
        local_ref[...],
        reach_ref[...],
    )
    hit = slot >= 0.0
    sigmoids = jnp.where(hit, jax.nn.sigmoid(logit_ref[...]), 0.0)
    total = jnp.sum(sigmoids, axis=0, keepdims=True)
    prob = sigmoids / total
    value = jnp.zeros((experts, tok), jnp.float32)
    for at in range(capacity):
        value = jnp.where(slot == float(at), returned[:, at : at + 1], value)
    own_values = own_ref[...] + jnp.sum(prob * value, axis=0, keepdims=True)
    mask = mask_ref[...].astype(jnp.float32)
    error = own_values - white
    value_error = mask * error
    weight = value_error * prob
    prob_grad = value_error * value
    sigma = (prob_grad - jnp.sum(prob_grad * prob, axis=0, keepdims=True)) / total
    chosen = sigma * sigmoids * (1.0 - sigmoids)
    lane = lax.broadcasted_iota(jnp.int32, (experts, 128), 1)
    message = jnp.zeros((experts, 128), jnp.float32)
    for at in range(capacity):
        here = slot == float(at)
        first = jnp.sum(jnp.where(here, weight, 0.0), axis=1, keepdims=True)
        second = jnp.sum(jnp.where(here, chosen, 0.0), axis=1, keepdims=True)
        message = jnp.where(lane == at, first, message)
        message = jnp.where(lane == capacity + at, second, message)
    out_ref[...] = jnp.broadcast_to(message[:, None, :], out_ref.shape)
    val_ref[...] = own_values
    err_ref[...] = value_error
    loss = 0.5 * jnp.sum(mask * error * error, axis=1, keepdims=True)
    loss_ref[...] = jnp.broadcast_to(loss, loss_ref.shape)
    div_ref[...] = jnp.broadcast_to(divisor, div_ref.shape)


def delta_kernel(slots, turns, block_ref, got_ref, *refs):
    count = 1 + turns[-1][-1][0]
    gates, ups, hiddens = refs[:count], refs[count : 2 * count], refs[2 * count : 3 * count]
    delta_ref, spread_ref, split_ref = refs[3 * count :]
    expert_count, _, _ = got_ref.shape
    capacity = slots * len(turns)
    lanes = expert_count * slots
    hidden = gates[0].shape[0]
    lane = lax.broadcasted_iota(jnp.int32, (8, lanes), 1)
    row = lax.broadcasted_iota(jnp.int32, (8, lanes), 0)
    total = jnp.zeros((hidden, lanes), jnp.float32)
    for turn, held in enumerate(turns):
        tables = []
        for kind in range(2):
            table = jnp.zeros((8, lanes), jnp.float32)
            for expert in range(expert_count):
                shift = (expert * slots - kind * capacity - turn * slots) % 128
                got = got_ref[expert]
                moved = pltpu.roll(got, shift, 1) if shift else got
                table = jnp.where(
                    (lane >= expert * slots) & (lane < (expert + 1) * slots), moved, table
                )
            tables.append(table)
        found = [(which, at) for which, many in held for at in range(many)]
        for at, (which, within) in enumerate(found):
            here = row == block_ref[at]
            weight = jnp.sum(jnp.where(here, tables[0], 0.0), axis=0, keepdims=True)
            chosen = jnp.sum(jnp.where(here, tables[1], 0.0), axis=0, keepdims=True)
            into = slice((turn * 8 + at) * lanes, (turn * 8 + at + 1) * lanes)
            span = slice(within * lanes, (within + 1) * lanes)
            high = chosen.astype(jnp.bfloat16)
            rest = chosen - high.astype(jnp.float32)
            middle = rest.astype(jnp.bfloat16)
            low = rest - middle.astype(jnp.float32)
            split = jnp.where(row == 0, high.astype(jnp.float32), 0.0)
            split = jnp.where(row == 1, middle.astype(jnp.float32), split)
            split = jnp.where(row == 2, low, split)
            split_ref[:, into] = split.astype(jnp.bfloat16)
            total = total + hiddens[which][:, span].astype(jnp.float32) * weight
            delta_ref[0:hidden, into] = (gates[which][:, span] * weight).astype(jnp.bfloat16)
            delta_ref[hidden : 2 * hidden, into] = (ups[which][:, span] * weight).astype(
                jnp.bfloat16
            )
    spread_ref[...] = jnp.sum(total, axis=1, keepdims=True)


def local_call(kernel, out_shape, *arrays, smem=()):
    vmem = pl.BlockSpec(memory_space=pltpu.VMEM)
    scalar = pl.BlockSpec(memory_space=pltpu.SMEM)
    return pl.pallas_call(
        kernel,
        out_shape=out_shape,
        in_specs=[scalar if at in smem else vmem for at in range(len(arrays))],
        out_specs=jax.tree.map(lambda _: vmem, out_shape),
        cost_estimate=pl.CostEstimate(flops=1 << 20, bytes_accessed=1 << 21, transcendentals=0),
    )(*arrays)


def shaped(*shape, dtype=jnp.float32):
    return jax.ShapeDtypeStruct(shape, dtype)


def shards(
    tokens,
    norm_gain,
    router_weight,
    value_weight,
    gate_weight,
    up_weight,
    down_weight,
    routes,
    segment_ids,
    loss_mask,
    penalty_reward,
    scores,
):
    tok_count = tokens.shape[1]
    model_width = tokens.shape[2]
    experts = router_weight.shape[0]
    hidden_width = gate_weight.shape[1]
    dp_count = lax.axis_size("dp")
    expert_count = lax.axis_size("expert")
    capacity = tok_count * routes.shape[2] * 3 // (2 * experts)
    slots = capacity // chunks
    block_rows = expert_count * slots
    own_tokens = tokens[0]
    own_routes = routes[0]
    normed = norm_rows(own_tokens, norm_gain)
    expert_ids = jnp.arange(experts, dtype=jnp.int32)[:, None]
    hit = (own_routes[:, 0][None, :] == expert_ids) | (own_routes[:, 1][None, :] == expert_ids)
    before = jnp.arange(tok_count)[:, None] < jnp.arange(tok_count)[None, :]
    counted = lax.dot_general(
        hit.astype(jnp.bfloat16),
        before.astype(jnp.bfloat16),
        plain,
        preferred_element_type=jnp.float32,
    )
    slot_of = jnp.where(hit, counted, -1.0)
    placed = slot_of[:, None, :] == jnp.arange(capacity, dtype=jnp.float32)[None, :, None]
    down_float = down_weight[0].astype(jnp.float32)
    value_along = jnp.sum(down_float * value_weight[None, :], axis=1, keepdims=True)
    blocks = jnp.stack(relative_blocks(dp_count)).astype(jnp.int32)
    place = lax.axis_index("expert") * dp_count + lax.axis_index("dp")
    place = place.astype(jnp.int32).reshape(1)
    marker = passed_along(segment_ids[:, :1] + 1, "expert", -1)
    own_stats, local_return, reach = local_call(
        first_kernel,
        (shaped(1, 128), shaped(1, tok_count), shaped(1, tok_count)),
        segment_ids,
        loss_mask,
        penalty_reward,
        scores,
        marker,
    )
    rows, turns, made = None, [], []
    all_rows = capacity * expert_count * dp_count
    for turn in range(chunks):
        chosen = placed[:, turn * slots : (turn + 1) * slots].astype(jnp.bfloat16)
        sent = lax.dot_general(
            chosen.reshape(experts * slots, tok_count),
            normed,
            plain,
            preferred_element_type=jnp.bfloat16,
        ).reshape(experts, slots, model_width)
        got = lax.all_to_all(sent, "expert", split_axis=0, concat_axis=0, tiled=True)
        near, far = ring(got.reshape(block_rows, model_width), dp_count)
        held = [near, far] if turn == chunks - 1 else [near + far]
        turns.append([])
        offset = turn * dp_count * block_rows
        for pieces in held:
            rows, *results = forward(
                pieces, gate_weight[0], up_weight[0], value_along, rows, offset, all_rows
            )
            many = results[-1].shape[1] // block_rows
            offset += many * block_rows
            turns[-1].append((len(made), many))
            made.append(results)
    gates, ups, hiddens, partials = zip(*made)
    width = model_width // dp_count
    own_part = lax.dynamic_slice_in_dim(rows, lax.axis_index("dp") * width, width, axis=1)
    logits = lax.dot_general(
        router_weight, normed.astype(jnp.float32), last_last, precision=highest
    )
    token_value = jnp.sum(own_tokens.astype(jnp.float32) * value_weight[None, :], axis=1)

    outward = local_call(
        functools.partial(pack_kernel, expert_count, slots, turns),
        shaped(expert_count, dp_count, 128),
        blocks,
        *partials,
        own_stats,
        smem=(0,),
    )
    everyone = dp_count * expert_count
    inward = lax.all_to_all(
        outward.reshape(everyone, 128), ("expert", "dp"), 0, 0, tiled=True
    )
    tables, own_values, value_error, loss_part, divisor = local_call(
        functools.partial(value_kernel, capacity),
        (
            shaped(experts, dp_count, 128),
            shaped(1, tok_count),
            shaped(1, tok_count),
            shaped(dp_count, 128),
            shaped(1, 128),
        ),
        place,
        inward.reshape(expert_count, dp_count, 128),
        slot_of,
        logits,
        token_value[None],
        local_return,
        reach,
        loss_mask,
        smem=(0,),
    )
    owned = lax.all_to_all(
        tables.reshape(everyone, 128), ("expert", "dp"), 0, 0, tiled=True
    )
    token_part = jnp.sum(own_tokens.astype(jnp.float32) * value_error.reshape(tok_count, 1), axis=0)
    delta, spread, split = local_call(
        functools.partial(delta_kernel, slots, turns),
        (
            shaped(2 * hidden_width, all_rows, dtype=jnp.bfloat16),
            shaped(hidden_width, 1),
            shaped(8, all_rows, dtype=jnp.bfloat16),
        ),
        blocks,
        owned.reshape(expert_count, dp_count, 128),
        *gates,
        *ups,
        *hiddens,
        smem=(0,),
    )
    tile = model_width // 8
    both_grad = grads(delta, rows, tile, 0, 4, ())
    gate_grad, up_grad = grads(delta, rows, tile, 4, 4, both_grad)
    router_row = lax.dot_general(split, own_part, plain, preferred_element_type=jnp.float32)
    router_row = jnp.sum(router_row, axis=0, keepdims=True)
    down_grad = (spread * value_weight[None, :]).astype(jnp.bfloat16)
    value_part = token_part + jnp.sum(down_float * spread, axis=0)
    parted = jnp.concatenate([value_part.reshape(dp_count, width), loss_part], axis=1)
    parted = lax.all_to_all(parted, "dp", 0, 0, tiled=True)
    parted = jnp.sum(parted, axis=0, keepdims=True)
    last = to_all(jnp.concatenate([parted, router_row], axis=1), "expert")[:, 0]
    value_own = jnp.sum(last[:, : width + 128], axis=0, keepdims=True)
    mean_loss = value_own[0, width] / divisor[0, 0]
    final = to_all(jnp.concatenate([last[:, width + 128 :], value_own[:, :width]], axis=0), "dp")
    final = final.transpose(1, 0, 2).reshape(experts + 1, model_width)
    return (
        own_values,
        mean_loss,
        final[experts],
        final[:experts],
        gate_grad[None],
        up_grad[None],
        down_grad[None],
    )


def solution(mesh):
    placed = (
        P("dp", "expert", None),
        P(),
        P(),
        P(),
        P("expert", "dp", None),
        P("expert", "dp", None),
        P("expert", "dp", None),
        P("dp", "expert", None),
        P("dp", "expert"),
        P("dp", "expert"),
        P("dp", "expert"),
        P("dp", None),
    )

    return jax.shard_map(
        shards,
        mesh=mesh,
        in_specs=placed,
        out_specs=(
            P("dp", "expert"),
            P(),
            P(),
            P(),
            P("expert", "dp", None),
            P("expert", "dp", None),
            P("expert", "dp", None),
        ),
        check_vma=False,
    )
```

```python
import functools

import functools

import jax
import jax.numpy as jnp
from jax import lax
from jax.experimental import pallas as pl
from jax.experimental.pallas import tpu as pltpu
from jax.sharding import PartitionSpec as P


discount_rate = 0.9995
norm_epsilon = 1e-06
white_epsilon = 1e-05
highest = lax.Precision.HIGHEST
shares = (1, 1, 1)
stat_lane = 64
most_vmem = 67043328
forward_vmem = 40 << 20
last_last = (((1,), (1,)), ((), ()))
plain = (((1,), (0,)), ((), ()))


def to_all(array, axis):
    size = lax.axis_size(axis)
    return lax.all_to_all(
        jnp.broadcast_to(array[None], (size,) + array.shape), axis, 0, 0, tiled=True
    )


def norm_rows(tokens, norm_gain):
    as_float = tokens.astype(jnp.float32)
    inverse_rms = lax.rsqrt(jnp.mean(as_float * as_float, axis=-1, keepdims=True) + norm_epsilon)
    return (as_float * inverse_rms * norm_gain).astype(jnp.bfloat16)


def ring(block, dp_count):
    half = block.shape[0] // 2
    up = [(i, (i + 2) % dp_count) for i in range(dp_count)]
    down = [(i, (i - 2) % dp_count) for i in range(dp_count)]
    other = [(i, i ^ 1) for i in range(dp_count)]
    below = lax.ppermute(block, "dp", up)
    above = lax.ppermute(block, "dp", down)
    far_first = lax.ppermute(below[:half], "dp", up)
    far_second = lax.ppermute(above[half:], "dp", down)
    near, far = [block, below, above], [far_first, far_second]
    near_twins = [lax.ppermute(piece, "dp", other) for piece in near]
    far_twins = [lax.ppermute(piece, "dp", other) for piece in far]
    return near + near_twins, far + far_twins


def relative_blocks(dp_count):
    place = lax.axis_index("dp")
    chip, core = place // 2, place % 2
    chips = dp_count // 2
    places = [(twin, shift) for twin in (0, 1) for shift in (0, chips - 1, 1)] + [(0, 2), (1, 2)]
    return [((chip + shift) % chips) * 2 + (core ^ twin) for twin, shift in places]


def first_kernel(seg_ref, mask_ref, pen_ref, score_ref, own_ref, open_ref, reach_ref, shut_ref):
    tok = seg_ref.shape[1]
    segment = seg_ref[...].astype(jnp.float32)
    last = segment[:, tok - 1 :]
    lane = lax.broadcasted_iota(jnp.int32, (1, tok), 1).astype(jnp.float32)
    side = jnp.transpose(jnp.broadcast_to(segment, (tok, tok)))
    at_row = lax.broadcasted_iota(jnp.int32, (tok, tok), 0).astype(jnp.float32)
    at_lane = lax.broadcasted_iota(jnp.int32, (tok, tok), 1).astype(jnp.float32)
    same = side == jnp.broadcast_to(segment, (tok, tok))
    goes_on = jnp.sum(
        jnp.where(same & (at_row == at_lane + 1.0), 1.0, 0.0), axis=0, keepdims=True
    )
    picked = jnp.zeros((1, tok), jnp.float32)
    for which in range(score_ref.shape[1]):
        picked = picked + jnp.where(
            segment == float(which), score_ref[:, which : which + 1], 0.0
        )
    at_end = lane == tok - 1.0
    shut_reward = pen_ref[...] + jnp.where(goes_on == 0.0, picked, 0.0)
    open_reward = jnp.where(at_end, pen_ref[...], shut_reward)
    log_rate = jnp.log(jnp.float32(discount_rate))
    ahead = at_row - at_lane
    discount = jnp.where(same & (ahead >= 0.0), jnp.exp(ahead * log_rate), 0.0)

    def summed(reward):
        column = jnp.transpose(jnp.broadcast_to(reward, (tok, tok)))
        return jnp.sum(discount * column, axis=0, keepdims=True)

    shut, opened = summed(shut_reward), summed(open_reward)
    reach = jnp.where(segment == last, jnp.exp((tok - lane) * log_rate), 0.0)
    mask = mask_ref[...].astype(jnp.float32)
    count = jnp.sum(mask, axis=1, keepdims=True)
    safe = jnp.maximum(count, 1.0)

    def over(values):
        return jnp.sum(mask * values, axis=1, keepdims=True)

    mean_open, mean_reach, mean_shut = over(opened) / safe, over(reach) / safe, over(shut) / safe
    off_open, off_reach, off_shut = opened - mean_open, reach - mean_reach, shut - mean_shut
    parts = [
        count,
        segment[:, :1],
        last,
        reach[:, :1],
        opened[:, :1],
        mean_open,
        mean_reach,
        over(off_open * off_open),
        over(off_open * off_reach),
        over(off_reach * off_reach),
        shut[:, :1],
        mean_shut,
        over(off_shut * off_shut),
    ]
    own = jnp.zeros((1, 128), jnp.float32)
    spot = lax.broadcasted_iota(jnp.int32, (1, 128), 1)
    for at, part in enumerate(parts):
        own = jnp.where(spot == stat_lane + at, part, own)
    own_ref[...] = own
    open_ref[...] = opened
    reach_ref[...] = reach
    shut_ref[...] = shut


def whiten(everyone, stride, place, opened, reach, shut):
    size = everyone.shape[0]
    table = jnp.transpose(everyone)[stat_lane : stat_lane + 16]
    (counts, first, last, factor, term, mean_open, mean_reach, square_open, square_mixed,
     square_reach, shut_term, mean_shut, square_shut) = [table[at : at + 1] for at in range(13)]
    lane = lax.broadcasted_iota(jnp.int32, (1, size), 1)
    inner = lane + stride < size
    goes_on = inner & (last == pltpu.roll(first, size - stride, 1))
    factor = jnp.where(goes_on, factor, 0.0)
    term = jnp.where(goes_on, term, shut_term)
    step = stride
    while step < size:
        inside = lane + step < size
        next_factor = jnp.where(inside, pltpu.roll(factor, size - step, 1), 1.0)
        next_term = jnp.where(inside, pltpu.roll(term, size - step, 1), 0.0)
        term = term + factor * next_term
        factor = factor * next_factor
        step *= 2
    carry = jnp.where(goes_on, pltpu.roll(term, size - stride, 1), 0.0)
    means = jnp.where(goes_on, mean_open + mean_reach * carry, mean_shut)
    squares = jnp.where(
        goes_on,
        square_open + 2.0 * carry * square_mixed + carry * carry * square_reach,
        square_shut,
    )
    total = jnp.sum(counts, axis=1, keepdims=True)
    divisor = jnp.maximum(total, 1.0)
    centre = jnp.sum(counts * means, axis=1, keepdims=True) / divisor
    apart = means - centre
    square = jnp.sum(squares + counts * apart * apart, axis=1, keepdims=True)
    mine = lane == place
    here = jnp.sum(jnp.where(mine, carry, 0.0), axis=1, keepdims=True)
    onward = jnp.sum(jnp.where(mine & goes_on, 1.0, 0.0), axis=1, keepdims=True)
    returns = jnp.where(onward > 0.0, opened + reach * here, shut)
    return (returns - centre) * lax.rsqrt(square / divisor + white_epsilon), divisor


def end_kernel(final_ref, router_ref, value_ref):
    count, rows, width = final_ref.shape
    for at in range(count):
        span = slice(at * width, (at + 1) * width)
        router_ref[:, span] = final_ref[at, : rows - 1]
        value_ref[:, span] = final_ref[at, rows - 1 :]


def forward_kernel(count, chained, offset, *refs):
    pieces = refs[:count]
    gate_ref, up_ref, along_ref = refs[count : count + 3]
    refs = refs[count + 3 + chained :]
    rows_ref, gates_out, ups_out, hidden_out, part_ref = refs[:5]
    held, gates_ref, ups_ref, hidden_ref, into, out, done = refs[5:]
    copies = []
    start = 0
    for at, piece in enumerate(pieces):
        span = piece.shape[0]
        copy = pltpu.make_async_copy(piece, held.at[pl.ds(start, span)], into.at[at])
        copy.start()
        copies.append(copy)
        start += span
    for copy in copies:
        copy.wait()
    back = pltpu.make_async_copy(held, rows_ref.at[pl.ds(offset, start)], out)
    back.start()
    pair = 256

    @pl.loop(0, start // pair)
    def _(turn):
        at = pl.multiple_of(turn * pair, pair)
        rows = held[pl.ds(at, pair), :]
        gate = lax.dot_general(
            gate_ref[...], rows, last_last, preferred_element_type=jnp.float32
        )
        up = lax.dot_general(up_ref[...], rows, last_last, preferred_element_type=jnp.float32)
        along = along_ref[...]
        sig = jax.nn.sigmoid(gate)
        swish = gate * sig
        hidden = (swish * up).astype(jnp.bfloat16)
        gates_ref[:, pl.ds(at, pair)] = along * up * sig * (1.0 + gate * (1.0 - sig))
        ups_ref[:, pl.ds(at, pair)] = along * swish
        hidden_ref[:, pl.ds(at, pair)] = hidden
        part_ref[:, pl.ds(at, pair)] = jnp.sum(
            hidden.astype(jnp.float32) * along, axis=0, keepdims=True
        )

    leaving = [
        pltpu.make_async_copy(made, target, done.at[at])
        for at, (made, target) in enumerate(
            [(gates_ref, gates_out), (ups_ref, ups_out), (hidden_ref, hidden_out)]
        )
    ]
    for copy in leaving:
        copy.start()
    for copy in leaving:
        copy.wait()
    back.wait()


def forward(pieces, gate, up, along, rows, offset, all_rows):
    total = sum(piece.shape[0] for piece in pieces)
    width = pieces[0].shape[1]
    hidden = gate.shape[0]
    count = len(pieces)
    vmem = pl.BlockSpec(memory_space=pltpu.VMEM)
    far = pl.BlockSpec(memory_space=pltpu.HBM)
    chained = [] if rows is None else [rows]
    return pl.pallas_call(
        functools.partial(forward_kernel, count, len(chained), offset),
        out_shape=(
            jax.ShapeDtypeStruct((all_rows, width), jnp.bfloat16),
            jax.ShapeDtypeStruct((hidden, total), jnp.float32),
            jax.ShapeDtypeStruct((hidden, total), jnp.float32),
            jax.ShapeDtypeStruct((hidden, total), jnp.bfloat16),
            jax.ShapeDtypeStruct((1, total), jnp.float32),
        ),
        in_specs=[far] * count + [vmem] * 3 + [far] * len(chained),
        out_specs=(far, far, far, far, vmem),
        input_output_aliases={count + 3: 0} if chained else {},
        scratch_shapes=[
            pltpu.VMEM((total, width), jnp.bfloat16),
            pltpu.VMEM((hidden, total), jnp.float32),
            pltpu.VMEM((hidden, total), jnp.float32),
            pltpu.VMEM((hidden, total), jnp.bfloat16),
            pltpu.SemaphoreType.DMA((count,)),
            pltpu.SemaphoreType.DMA,
            pltpu.SemaphoreType.DMA((3,)),
        ],
        compiler_params=pltpu.CompilerParams(vmem_limit_bytes=forward_vmem),
        cost_estimate=pl.CostEstimate(
            flops=4 * total * width * hidden,
            bytes_accessed=4 * total * width + 4 * hidden * width,
            transcendentals=0,
        ),
    )(*pieces, gate, up, along, *chained)


def grad_kernel(chained, delta_ref, rows_ref, *refs):
    gate_ref, up_ref = refs[chained:]
    hidden = gate_ref.shape[0]
    both = lax.dot_general(
        delta_ref[...], rows_ref[...], plain, preferred_element_type=jnp.float32
    ).astype(jnp.bfloat16)
    gate_ref[...] = both[:hidden]
    up_ref[...] = both[hidden:]


def grads(delta, rows, tile, first, count, made):
    total, width = rows.shape
    hidden = delta.shape[0] // 2
    far = pl.BlockSpec(memory_space=pltpu.HBM)
    out = pl.BlockSpec((hidden, tile), lambda at: (0, at + first))
    return pl.pallas_call(
        functools.partial(grad_kernel, len(made)),
        grid=(count,),
        out_shape=(jax.ShapeDtypeStruct((hidden, width), jnp.bfloat16),) * 2,
        in_specs=[
            pl.BlockSpec(delta.shape, lambda at: (0, 0)),
            pl.BlockSpec((total, tile), lambda at: (0, at + first)),
        ]
        + [far] * len(made),
        out_specs=(out, out),
        input_output_aliases={2: 0, 3: 1} if made else {},
        compiler_params=pltpu.CompilerParams(vmem_limit_bytes=most_vmem),
        cost_estimate=pl.CostEstimate(
            flops=4 * total * hidden * tile * count,
            bytes_accessed=2 * total * tile * count,
            transcendentals=0,
        ),
    )(delta, rows, *made)


def pack_kernel(expert_count, turns, block_ref, *refs):
    parts, own_ref, out_ref = refs[:-2], refs[-2], refs[-1]
    own = jnp.broadcast_to(own_ref[...], (8, 128))
    ordered = []
    for slots, held in turns:
        lanes = expert_count * slots
        row = lax.broadcasted_iota(jnp.int32, (8, lanes), 0)
        total = jnp.zeros((8, lanes), jnp.float32)
        found = [(which, at) for which, many in held for at in range(many)]
        for at, (which, within) in enumerate(found):
            piece = parts[which][:, within * lanes : (within + 1) * lanes]
            total = jnp.where(row == block_ref[at], jnp.broadcast_to(piece, (8, lanes)), total)
        ordered.append(total)
    lane = lax.broadcasted_iota(jnp.int32, (8, 128), 1)
    for expert in range(expert_count):
        message = own
        base = 0
        for (slots, _), part in zip(turns, ordered):
            tile, first = divmod(expert * slots, 128)
            shift = (base - first) % 128
            moved = part[:, tile * 128 : (tile + 1) * 128]
            moved = pltpu.roll(moved, shift, 1) if shift else moved
            message = jnp.where((lane >= base) & (lane < base + slots), moved, message)
            base += slots
        out_ref[expert] = message


def value_kernel(
    capacity, place_ref, got_ref, slot_ref, logit_ref, own_ref, open_ref, reach_ref, shut_ref,
    mask_ref, out_ref, val_ref, err_ref, loss_ref, div_ref
):
    experts, tok = slot_ref.shape
    slot = slot_ref[...]
    got = got_ref[...]
    returned = jnp.sum(got, axis=1)
    stride = got.shape[1]
    white, divisor = whiten(
        got.reshape(got.shape[0] * stride, got.shape[2]),
        stride,
        place_ref[0],
        open_ref[...],
        reach_ref[...],
        shut_ref[...],
    )
    hit = slot >= 0.0
    sigmoids = jnp.where(hit, jax.nn.sigmoid(logit_ref[...]), 0.0)
    total = jnp.sum(sigmoids, axis=0, keepdims=True)
    prob = sigmoids / total
    value = jnp.zeros((experts, tok), jnp.float32)
    for at in range(capacity):
        value = jnp.where(slot == float(at), returned[:, at : at + 1], value)
    own_values = own_ref[...] + jnp.sum(prob * value, axis=0, keepdims=True)
    mask = mask_ref[...].astype(jnp.float32)
    error = own_values - white
    value_error = mask * error
    weight = value_error * prob
    prob_grad = value_error * value
    sigma = (prob_grad - jnp.sum(prob_grad * prob, axis=0, keepdims=True)) / total
    chosen = sigma * sigmoids * (1.0 - sigmoids)
    lane = lax.broadcasted_iota(jnp.int32, (experts, 128), 1)
    message = jnp.zeros((experts, 128), jnp.float32)
    for at in range(capacity):
        here = slot == float(at)
        first = jnp.sum(jnp.where(here, weight, 0.0), axis=1, keepdims=True)
        second = jnp.sum(jnp.where(here, chosen, 0.0), axis=1, keepdims=True)
        message = jnp.where(lane == at, first, message)
        message = jnp.where(lane == capacity + at, second, message)
    out_ref[...] = jnp.broadcast_to(message[:, None, :], out_ref.shape)
    val_ref[...] = own_values
    err_ref[...] = value_error
    loss = 0.5 * jnp.sum(mask * error * error, axis=1, keepdims=True)
    loss_ref[...] = jnp.broadcast_to(loss, loss_ref.shape)
    div_ref[...] = jnp.broadcast_to(divisor, div_ref.shape)


def delta_kernel(capacity, turns, block_ref, got_ref, *refs):
    count = 1 + turns[-1][1][-1][0]
    delta_ref, spread_ref, split_ref = refs[3 * count : 3 * count + 3]
    held, into = refs[3 * count + 3 : 6 * count + 3], refs[6 * count + 3]
    gates, ups, hiddens = held[:count], held[count : 2 * count], held[2 * count :]
    coming = [
        pltpu.make_async_copy(refs[at], held[at], into.at[at]) for at in range(3 * count)
    ]
    for which in range(count):
        for copy in coming[which::count]:
            copy.start()
    expert_count, _, _ = got_ref.shape
    hidden = spread_ref.shape[0]
    lane = lax.broadcasted_iota(jnp.int32, (8, 128), 1)
    row = lax.broadcasted_iota(jnp.int32, (8, 128), 0)
    total = jnp.zeros((hidden, 128), jnp.float32)
    base = start = 0
    for slots, owned in turns:
        tiles = expert_count * slots // 128
        tables = []
        for kind in range(2):
            for tile in range(tiles):
                table = jnp.zeros((8, 128), jnp.float32)
                for spot in range(0, 128, slots):
                    shift = (spot - kind * capacity - base) % 128
                    got = got_ref[(tile * 128 + spot) // slots]
                    moved = pltpu.roll(got, shift, 1) if shift else got
                    table = jnp.where((lane >= spot) & (lane < spot + slots), moved, table)
                tables.append(table)
        found = [(which, at) for which, many in owned for at in range(many)]
        for at, (which, within) in enumerate(found):
            if within == 0:
                for copy in coming[which::count]:
                    copy.wait()
            here = row == block_ref[at]
            for tile in range(tiles):
                weight = jnp.sum(jnp.where(here, tables[tile], 0.0), axis=0, keepdims=True)
                chosen = jnp.sum(
                    jnp.where(here, tables[tiles + tile], 0.0), axis=0, keepdims=True
                )
                into_at = slice(start, start + 128)
                start += 128
                from_at = slice(
                    (within * tiles + tile) * 128, (within * tiles + tile + 1) * 128
                )
                high = chosen.astype(jnp.bfloat16)
                rest = chosen - high.astype(jnp.float32)
                middle = rest.astype(jnp.bfloat16)
                low = rest - middle.astype(jnp.float32)
                split = jnp.where(row == 0, high.astype(jnp.float32), 0.0)
                split = jnp.where(row == 1, middle.astype(jnp.float32), split)
                split = jnp.where(row == 2, low, split)
                split_ref[:, into_at] = split.astype(jnp.bfloat16)
                total = total + hiddens[which][:, from_at].astype(jnp.float32) * weight
                delta_ref[0:hidden, into_at] = (gates[which][:, from_at] * weight).astype(
                    jnp.bfloat16
                )
                delta_ref[hidden : 2 * hidden, into_at] = (
                    ups[which][:, from_at] * weight
                ).astype(jnp.bfloat16)
        base += slots
    spread_ref[...] = jnp.sum(total, axis=1, keepdims=True)


def local_call(kernel, out_shape, *arrays, smem=(), hbm=(), scratch=(), limit=most_vmem):
    vmem = pl.BlockSpec(memory_space=pltpu.VMEM)
    scalar = pl.BlockSpec(memory_space=pltpu.SMEM)
    far = pl.BlockSpec(memory_space=pltpu.HBM)
    return pl.pallas_call(
        kernel,
        out_shape=out_shape,
        in_specs=[
            scalar if at in smem else far if at in hbm else vmem for at in range(len(arrays))
        ],
        out_specs=jax.tree.map(lambda _: vmem, out_shape),
        scratch_shapes=list(scratch),
        compiler_params=pltpu.CompilerParams(vmem_limit_bytes=limit),
        cost_estimate=pl.CostEstimate(flops=1 << 20, bytes_accessed=1 << 21, transcendentals=0),
    )(*arrays)


def shaped(*shape, dtype=jnp.float32):
    return jax.ShapeDtypeStruct(shape, dtype)


def shards(
    tokens,
    norm_gain,
    router_weight,
    value_weight,
    gate_weight,
    up_weight,
    down_weight,
    routes,
    segment_ids,
    loss_mask,
    penalty_reward,
    scores,
):
    tok_count = tokens.shape[1]
    model_width = tokens.shape[2]
    experts = router_weight.shape[0]
    hidden_width = gate_weight.shape[1]
    dp_count = lax.axis_size("dp")
    expert_count = lax.axis_size("expert")
    capacity = tok_count * routes.shape[2] * 3 // (2 * experts)
    own_tokens = tokens[0]
    own_routes = routes[0]
    normed = norm_rows(own_tokens, norm_gain)
    expert_ids = jnp.arange(experts, dtype=jnp.int32)[:, None]
    hit = (own_routes[:, 0][None, :] == expert_ids) | (own_routes[:, 1][None, :] == expert_ids)
    before = jnp.arange(tok_count)[:, None] < jnp.arange(tok_count)[None, :]
    counted = lax.dot_general(
        hit.astype(jnp.bfloat16),
        before.astype(jnp.bfloat16),
        plain,
        preferred_element_type=jnp.float32,
    )
    slot_of = jnp.where(hit, counted, -1.0)
    placed = slot_of[:, None, :] == jnp.arange(capacity, dtype=jnp.float32)[None, :, None]
    down_float = down_weight[0].astype(jnp.float32)
    value_along = jnp.sum(down_float * value_weight[None, :], axis=1, keepdims=True)
    blocks = jnp.stack(relative_blocks(dp_count)).astype(jnp.int32)
    place = lax.axis_index("expert") * dp_count + lax.axis_index("dp")
    place = place.astype(jnp.int32).reshape(1)
    own_stats, opened, reach, shut = local_call(
        first_kernel,
        (shaped(1, 128),) + (shaped(1, tok_count),) * 3,
        segment_ids,
        loss_mask,
        penalty_reward,
        scores,
    )
    rows, turns, made = None, [], []
    all_rows = capacity * expert_count * dp_count
    first = offset = 0
    for turn, share in enumerate(shares):
        slots = capacity * share // sum(shares)
        block_rows = expert_count * slots
        chosen = placed[:, first : first + slots].astype(jnp.bfloat16)
        first += slots
        sent = lax.dot_general(
            chosen.reshape(experts * slots, tok_count),
            normed,
            plain,
            preferred_element_type=jnp.bfloat16,
        ).reshape(experts, slots, model_width)
        got = lax.all_to_all(sent, "expert", split_axis=0, concat_axis=0, tiled=True)
        near, far = ring(got.reshape(block_rows, model_width), dp_count)
        turns.append((slots, []))
        held = [near, far] if turn == len(shares) - 1 else [near + far]
        for pieces in held:
            rows, *results = forward(
                pieces, gate_weight[0], up_weight[0], value_along, rows, offset, all_rows
            )
            many = results[-1].shape[1] // block_rows
            offset += many * block_rows
            turns[-1][1].append((len(made), many))
            made.append(results)
    gates, ups, hiddens, partials = zip(*made)
    width = model_width // dp_count
    own_part = lax.dynamic_slice_in_dim(rows, lax.axis_index("dp") * width, width, axis=1)
    logits = lax.dot_general(
        router_weight, normed.astype(jnp.float32), last_last, precision=highest
    )
    token_value = jnp.sum(own_tokens.astype(jnp.float32) * value_weight[None, :], axis=1)

    outward = local_call(
        functools.partial(pack_kernel, expert_count, turns),
        shaped(expert_count, dp_count, 128),
        blocks,
        *partials,
        own_stats,
        smem=(0,),
    )
    everyone = dp_count * expert_count
    inward = lax.all_to_all(
        outward.reshape(everyone, 128), ("expert", "dp"), 0, 0, tiled=True
    )
    tables, own_values, value_error, loss_part, divisor = local_call(
        functools.partial(value_kernel, capacity),
        (
            shaped(experts, dp_count, 128),
            shaped(1, tok_count),
            shaped(1, tok_count),
            shaped(dp_count, 128),
            shaped(1, 128),
        ),
        place,
        inward.reshape(expert_count, dp_count, 128),
        slot_of,
        logits,
        token_value[None],
        opened,
        reach,
        shut,
        loss_mask,
        smem=(0,),
    )
    owned = lax.all_to_all(
        tables.reshape(everyone, 128), ("expert", "dp"), 0, 0, tiled=True
    )
    token_part = jnp.sum(own_tokens.astype(jnp.float32) * value_error.reshape(tok_count, 1), axis=0)
    delta, spread, split = local_call(
        functools.partial(delta_kernel, capacity, turns),
        (
            shaped(2 * hidden_width, all_rows, dtype=jnp.bfloat16),
            shaped(hidden_width, 1),
            shaped(8, all_rows, dtype=jnp.bfloat16),
        ),
        blocks,
        owned.reshape(expert_count, dp_count, 128),
        *gates,
        *ups,
        *hiddens,
        smem=(0,),
        hbm=range(2, 2 + 3 * len(made)),
        scratch=[pltpu.VMEM(a.shape, a.dtype) for a in gates + ups + hiddens]
        + [pltpu.SemaphoreType.DMA((3 * len(made),))],
        limit=most_vmem,
    )
    tile = model_width // 8
    both_grad = grads(delta, rows, tile, 0, 4, ())
    gate_grad, up_grad = grads(delta, rows, tile, 4, 4, both_grad)
    router_row = lax.dot_general(split, own_part, plain, preferred_element_type=jnp.float32)
    router_row = jnp.sum(router_row, axis=0, keepdims=True)
    down_grad = (spread * value_weight[None, :]).astype(jnp.bfloat16)
    value_part = token_part + jnp.sum(down_float * spread, axis=0)
    parted = jnp.concatenate([value_part.reshape(dp_count, width), loss_part], axis=1)
    parted = lax.all_to_all(parted, "dp", 0, 0, tiled=True)
    parted = jnp.sum(parted, axis=0, keepdims=True)
    last = to_all(jnp.concatenate([parted, router_row], axis=1), "expert")[:, 0]
    value_own = jnp.sum(last[:, : width + 128], axis=0, keepdims=True)
    mean_loss = value_own[0, width] / divisor[0, 0]
    final = to_all(jnp.concatenate([last[:, width + 128 :], value_own[:, :width]], axis=0), "dp")
    router_grad, value_grad = local_call(
        end_kernel, (shaped(experts, model_width), shaped(1, model_width)), final
    )
    return (
        own_values,
        mean_loss,
        value_grad[0],
        router_grad,
        gate_grad[None],
        up_grad[None],
        down_grad[None],
    )


def solution(mesh):
    placed = (
        P("dp", "expert", None),
        P(),
        P(),
        P(),
        P("expert", "dp", None),
        P("expert", "dp", None),
        P("expert", "dp", None),
        P("dp", "expert", None),
        P("dp", "expert"),
        P("dp", "expert"),
        P("dp", "expert"),
        P("dp", None),
    )

    return jax.shard_map(
        shards,
        mesh=mesh,
        in_specs=placed,
        out_specs=(
            P("dp", "expert"),
            P(),
            P(),
            P(),
            P("expert", "dp", None),
            P("expert", "dp", None),
            P("expert", "dp", None),
        ),
        check_vma=False,
    )
```

```python
import functools

import functools

import jax
import jax.numpy as jnp
from jax import lax
from jax.experimental import pallas as pl
from jax.experimental.pallas import tpu as pltpu
from jax.sharding import PartitionSpec as P


discount_rate = 0.9995
norm_epsilon = 1e-06
white_epsilon = 1e-05
highest = lax.Precision.HIGHEST
shares = (1, 1, 1)
stat_lane = 64
joined_order = (0, 1, 2, 6, 3, 4, 5, 7)
most_vmem = 60 * 1024 * 1024
forward_vmem = 40 << 20
last_last = (((1,), (1,)), ((), ()))
plain = (((1,), (0,)), ((), ()))


def to_all(array, axis):
    size = lax.axis_size(axis)
    return lax.all_to_all(
        jnp.broadcast_to(array[None], (size,) + array.shape), axis, 0, 0, tiled=True
    )


def norm_rows(tokens, norm_gain):
    as_float = tokens.astype(jnp.float32)
    inverse_rms = lax.rsqrt(jnp.mean(as_float * as_float, axis=-1, keepdims=True) + norm_epsilon)
    return (as_float * inverse_rms * norm_gain).astype(jnp.bfloat16)


def ring(block, dp_count, split):
    half = block.shape[0] // 2
    up = [(i, (i + 2) % dp_count) for i in range(dp_count)]
    down = [(i, (i - 2) % dp_count) for i in range(dp_count)]
    other = [(i, i ^ 1) for i in range(dp_count)]
    below = lax.ppermute(block, "dp", up)
    above = lax.ppermute(block, "dp", down)
    far_first = lax.ppermute(below[:half], "dp", up)
    far_second = lax.ppermute(above[half:], "dp", down)
    near, far = [block, below, above], [far_first, far_second]
    if not split:
        whole = jnp.concatenate(near + far, axis=0)
        return [whole, lax.ppermute(whole, "dp", other)], []
    near_twins = [lax.ppermute(piece, "dp", other) for piece in near]
    whole = jnp.concatenate(far, axis=0)
    return near + near_twins, [whole, lax.ppermute(whole, "dp", other)]


def relative_blocks(dp_count):
    place = lax.axis_index("dp")
    chip, core = place // 2, place % 2
    chips = dp_count // 2
    places = [(twin, shift) for twin in (0, 1) for shift in (0, chips - 1, 1)] + [(0, 2), (1, 2)]
    return [((chip + shift) % chips) * 2 + (core ^ twin) for twin, shift in places]


def first_kernel(seg_ref, mask_ref, pen_ref, score_ref, own_ref, open_ref, reach_ref, shut_ref):
    tok = seg_ref.shape[1]
    segment = seg_ref[...].astype(jnp.float32)
    last = segment[:, tok - 1 :]
    lane = lax.broadcasted_iota(jnp.int32, (1, tok), 1).astype(jnp.float32)
    side = jnp.transpose(jnp.broadcast_to(segment, (tok, tok)))
    at_row = lax.broadcasted_iota(jnp.int32, (tok, tok), 0).astype(jnp.float32)
    at_lane = lax.broadcasted_iota(jnp.int32, (tok, tok), 1).astype(jnp.float32)
    same = side == jnp.broadcast_to(segment, (tok, tok))
    goes_on = jnp.sum(
        jnp.where(same & (at_row == at_lane + 1.0), 1.0, 0.0), axis=0, keepdims=True
    )
    picked = jnp.zeros((1, tok), jnp.float32)
    for which in range(score_ref.shape[1]):
        picked = picked + jnp.where(
            segment == float(which), score_ref[:, which : which + 1], 0.0
        )
    at_end = lane == tok - 1.0
    shut_reward = pen_ref[...] + jnp.where(goes_on == 0.0, picked, 0.0)
    open_reward = jnp.where(at_end, pen_ref[...], shut_reward)
    log_rate = jnp.log(jnp.float32(discount_rate))
    ahead = at_row - at_lane
    discount = jnp.where(same & (ahead >= 0.0), jnp.exp(ahead * log_rate), 0.0)

    def summed(reward):
        column = jnp.transpose(jnp.broadcast_to(reward, (tok, tok)))
        return jnp.sum(discount * column, axis=0, keepdims=True)

    shut, opened = summed(shut_reward), summed(open_reward)
    reach = jnp.where(segment == last, jnp.exp((tok - lane) * log_rate), 0.0)
    mask = mask_ref[...].astype(jnp.float32)
    count = jnp.sum(mask, axis=1, keepdims=True)
    safe = jnp.maximum(count, 1.0)

    def over(values):
        return jnp.sum(mask * values, axis=1, keepdims=True)

    mean_open, mean_reach, mean_shut = over(opened) / safe, over(reach) / safe, over(shut) / safe
    off_open, off_reach, off_shut = opened - mean_open, reach - mean_reach, shut - mean_shut
    parts = [
        count,
        segment[:, :1],
        last,
        reach[:, :1],
        opened[:, :1],
        mean_open,
        mean_reach,
        over(off_open * off_open),
        over(off_open * off_reach),
        over(off_reach * off_reach),
        shut[:, :1],
        mean_shut,
        over(off_shut * off_shut),
    ]
    own = jnp.zeros((1, 128), jnp.float32)
    spot = lax.broadcasted_iota(jnp.int32, (1, 128), 1)
    for at, part in enumerate(parts):
        own = jnp.where(spot == stat_lane + at, part, own)
    own_ref[...] = own
    open_ref[...] = opened
    reach_ref[...] = reach
    shut_ref[...] = shut


def whiten(everyone, stride, place, opened, reach, shut):
    size = everyone.shape[0]
    table = jnp.transpose(everyone)[stat_lane : stat_lane + 16]
    (counts, first, last, factor, term, mean_open, mean_reach, square_open, square_mixed,
     square_reach, shut_term, mean_shut, square_shut) = [table[at : at + 1] for at in range(13)]
    lane = lax.broadcasted_iota(jnp.int32, (1, size), 1)
    inner = lane + stride < size
    goes_on = inner & (last == pltpu.roll(first, size - stride, 1))
    factor = jnp.where(goes_on, factor, 0.0)
    term = jnp.where(goes_on, term, shut_term)
    step = stride
    while step < size:
        inside = lane + step < size
        next_factor = jnp.where(inside, pltpu.roll(factor, size - step, 1), 1.0)
        next_term = jnp.where(inside, pltpu.roll(term, size - step, 1), 0.0)
        term = term + factor * next_term
        factor = factor * next_factor
        step *= 2
    carry = jnp.where(goes_on, pltpu.roll(term, size - stride, 1), 0.0)
    means = jnp.where(goes_on, mean_open + mean_reach * carry, mean_shut)
    squares = jnp.where(
        goes_on,
        square_open + 2.0 * carry * square_mixed + carry * carry * square_reach,
        square_shut,
    )
    total = jnp.sum(counts, axis=1, keepdims=True)
    divisor = jnp.maximum(total, 1.0)
    centre = jnp.sum(counts * means, axis=1, keepdims=True) / divisor
    apart = means - centre
    square = jnp.sum(squares + counts * apart * apart, axis=1, keepdims=True)
    mine = lane == place
    here = jnp.sum(jnp.where(mine, carry, 0.0), axis=1, keepdims=True)
    onward = jnp.sum(jnp.where(mine & goes_on, 1.0, 0.0), axis=1, keepdims=True)
    returns = jnp.where(onward > 0.0, opened + reach * here, shut)
    return (returns - centre) * lax.rsqrt(square / divisor + white_epsilon), divisor


def end_kernel(final_ref, router_ref, value_ref):
    count, rows, width = final_ref.shape
    for at in range(count):
        span = slice(at * width, (at + 1) * width)
        router_ref[:, span] = final_ref[at, : rows - 1]
        value_ref[:, span] = final_ref[at, rows - 1 :]


def forward_kernel(count, chained, offset, *refs):
    pieces = refs[:count]
    gate_ref, up_ref, along_ref = refs[count : count + 3]
    refs = refs[count + 3 + chained :]
    rows_ref, gates_ref, ups_ref, hidden_ref, part_ref, held, into, out = refs
    copies = []
    start = 0
    for at, piece in enumerate(pieces):
        span = piece.shape[0]
        copy = pltpu.make_async_copy(piece, held.at[pl.ds(start, span)], into.at[at])
        copy.start()
        copies.append(copy)
        start += span
    for copy in copies:
        copy.wait()
    back = pltpu.make_async_copy(held, rows_ref.at[pl.ds(offset, start)], out)
    back.start()
    pair = 256

    @pl.loop(0, start // pair)
    def _(turn):
        at = pl.multiple_of(turn * pair, pair)
        rows = held[pl.ds(at, pair), :]
        gate = lax.dot_general(
            gate_ref[...], rows, last_last, preferred_element_type=jnp.float32
        )
        up = lax.dot_general(up_ref[...], rows, last_last, preferred_element_type=jnp.float32)
        along = along_ref[...]
        sig = jax.nn.sigmoid(gate)
        swish = gate * sig
        hidden = (swish * up).astype(jnp.bfloat16)
        gates_ref[:, pl.ds(at, pair)] = along * up * sig * (1.0 + gate * (1.0 - sig))
        ups_ref[:, pl.ds(at, pair)] = along * swish
        hidden_ref[:, pl.ds(at, pair)] = hidden
        part_ref[:, pl.ds(at, pair)] = jnp.sum(
            hidden.astype(jnp.float32) * along, axis=0, keepdims=True
        )

    back.wait()


def forward(pieces, gate, up, along, rows, offset, all_rows):
    total = sum(piece.shape[0] for piece in pieces)
    width = pieces[0].shape[1]
    hidden = gate.shape[0]
    count = len(pieces)
    vmem = pl.BlockSpec(memory_space=pltpu.VMEM)
    far = pl.BlockSpec(memory_space=pl.ANY)
    chained = [] if rows is None else [rows]
    return pl.pallas_call(
        functools.partial(forward_kernel, count, len(chained), offset),
        out_shape=(
            jax.ShapeDtypeStruct((all_rows, width), jnp.bfloat16),
            jax.ShapeDtypeStruct((hidden, total), jnp.float32),
            jax.ShapeDtypeStruct((hidden, total), jnp.float32),
            jax.ShapeDtypeStruct((hidden, total), jnp.bfloat16),
            jax.ShapeDtypeStruct((1, total), jnp.float32),
        ),
        in_specs=[far] * count + [vmem] * 3 + [far] * len(chained),
        out_specs=(far, vmem, vmem, vmem, vmem),
        input_output_aliases={count + 3: 0} if chained else {},
        scratch_shapes=[
            pltpu.VMEM((total, width), jnp.bfloat16),
            pltpu.SemaphoreType.DMA((count,)),
            pltpu.SemaphoreType.DMA,
        ],
        compiler_params=pltpu.CompilerParams(vmem_limit_bytes=forward_vmem),
        cost_estimate=pl.CostEstimate(
            flops=4 * total * width * hidden,
            bytes_accessed=4 * total * width + 4 * hidden * width,
            transcendentals=0,
        ),
    )(*pieces, gate, up, along, *chained)


def grad_kernel(chained, delta_ref, rows_ref, *refs):
    gate_ref, up_ref = refs[chained:]
    hidden = gate_ref.shape[0]
    both = lax.dot_general(
        delta_ref[...], rows_ref[...], plain, preferred_element_type=jnp.float32
    ).astype(jnp.bfloat16)
    gate_ref[...] = both[:hidden]
    up_ref[...] = both[hidden:]


def grads(delta, rows, tile, first, count, made):
    total, width = rows.shape
    hidden = delta.shape[0] // 2
    far = pl.BlockSpec(memory_space=pltpu.HBM)
    out = pl.BlockSpec((hidden, tile), lambda at: (0, at + first))
    return pl.pallas_call(
        functools.partial(grad_kernel, len(made)),
        grid=(count,),
        out_shape=(jax.ShapeDtypeStruct((hidden, width), jnp.bfloat16),) * 2,
        in_specs=[
            pl.BlockSpec(delta.shape, lambda at: (0, 0)),
            pl.BlockSpec((total, tile), lambda at: (0, at + first)),
        ]
        + [far] * len(made),
        out_specs=(out, out),
        input_output_aliases={2: 0, 3: 1} if made else {},
        compiler_params=pltpu.CompilerParams(vmem_limit_bytes=forward_vmem),
        cost_estimate=pl.CostEstimate(
            flops=4 * total * hidden * tile * count,
            bytes_accessed=2 * total * tile * count,
            transcendentals=0,
        ),
    )(delta, rows, *made)


def pack_kernel(expert_count, turns, block_ref, *refs):
    parts, own_ref, out_ref = refs[:-2], refs[-2], refs[-1]
    own = jnp.broadcast_to(own_ref[...], (8, 128))
    ordered = []
    for slots, held in turns:
        lanes = expert_count * slots
        row = lax.broadcasted_iota(jnp.int32, (8, lanes), 0)
        total = jnp.zeros((8, lanes), jnp.float32)
        found = [(which, at) for which, many in held for at in range(many)]
        for at, (which, within) in enumerate(found):
            piece = parts[which][:, within * lanes : (within + 1) * lanes]
            at = at if len(held) > 1 else joined_order[at]
            total = jnp.where(row == block_ref[at], jnp.broadcast_to(piece, (8, lanes)), total)
        ordered.append(total)
    lane = lax.broadcasted_iota(jnp.int32, (8, 128), 1)
    for expert in range(expert_count):
        message = own
        base = 0
        for (slots, _), part in zip(turns, ordered):
            tile, first = divmod(expert * slots, 128)
            shift = (base - first) % 128
            moved = part[:, tile * 128 : (tile + 1) * 128]
            moved = pltpu.roll(moved, shift, 1) if shift else moved
            message = jnp.where((lane >= base) & (lane < base + slots), moved, message)
            base += slots
        out_ref[expert] = message


def value_kernel(
    capacity, place_ref, got_ref, slot_ref, logit_ref, own_ref, open_ref, reach_ref, shut_ref,
    mask_ref, out_ref, val_ref, err_ref, loss_ref, div_ref
):
    experts, tok = slot_ref.shape
    slot = slot_ref[...]
    got = got_ref[...]
    returned = jnp.sum(got, axis=1)
    stride = got.shape[1]
    white, divisor = whiten(
        got.reshape(got.shape[0] * stride, got.shape[2]),
        stride,
        place_ref[0],
        open_ref[...],
        reach_ref[...],
        shut_ref[...],
    )
    hit = slot >= 0.0
    sigmoids = jnp.where(hit, jax.nn.sigmoid(logit_ref[...]), 0.0)
    total = jnp.sum(sigmoids, axis=0, keepdims=True)
    prob = sigmoids / total
    value = jnp.zeros((experts, tok), jnp.float32)
    for at in range(capacity):
        value = jnp.where(slot == float(at), returned[:, at : at + 1], value)
    own_values = own_ref[...] + jnp.sum(prob * value, axis=0, keepdims=True)
    mask = mask_ref[...].astype(jnp.float32)
    error = own_values - white
    value_error = mask * error
    weight = value_error * prob
    prob_grad = value_error * value
    sigma = (prob_grad - jnp.sum(prob_grad * prob, axis=0, keepdims=True)) / total
    chosen = sigma * sigmoids * (1.0 - sigmoids)
    lane = lax.broadcasted_iota(jnp.int32, (experts, 128), 1)
    message = jnp.zeros((experts, 128), jnp.float32)
    for at in range(capacity):
        here = slot == float(at)
        first = jnp.sum(jnp.where(here, weight, 0.0), axis=1, keepdims=True)
        second = jnp.sum(jnp.where(here, chosen, 0.0), axis=1, keepdims=True)
        message = jnp.where(lane == at, first, message)
        message = jnp.where(lane == capacity + at, second, message)
    out_ref[...] = jnp.broadcast_to(message[:, None, :], out_ref.shape)
    val_ref[...] = own_values
    err_ref[...] = value_error
    loss = 0.5 * jnp.sum(mask * error * error, axis=1, keepdims=True)
    loss_ref[...] = jnp.broadcast_to(loss, loss_ref.shape)
    div_ref[...] = jnp.broadcast_to(divisor, div_ref.shape)


def delta_kernel(capacity, turns, block_ref, got_ref, *refs):
    count = 1 + turns[-1][1][-1][0]
    delta_ref, spread_ref, split_ref = refs[3 * count : 3 * count + 3]
    held, into = refs[3 * count + 3 : 6 * count + 3], refs[6 * count + 3]
    gates, ups, hiddens = held[:count], held[count : 2 * count], held[2 * count :]
    coming = [
        pltpu.make_async_copy(refs[at], held[at], into.at[at]) for at in range(3 * count)
    ]
    for which in range(count):
        for copy in coming[which::count]:
            copy.start()
    expert_count, _, _ = got_ref.shape
    hidden = spread_ref.shape[0]
    lane = lax.broadcasted_iota(jnp.int32, (8, 128), 1)
    row = lax.broadcasted_iota(jnp.int32, (8, 128), 0)
    total = jnp.zeros((hidden, 128), jnp.float32)
    base = start = 0
    for slots, owned in turns:
        tiles = expert_count * slots // 128
        tables = []
        for kind in range(2):
            for tile in range(tiles):
                table = jnp.zeros((8, 128), jnp.float32)
                for spot in range(0, 128, slots):
                    shift = (spot - kind * capacity - base) % 128
                    got = got_ref[(tile * 128 + spot) // slots]
                    moved = pltpu.roll(got, shift, 1) if shift else got
                    table = jnp.where((lane >= spot) & (lane < spot + slots), moved, table)
                tables.append(table)
        found = [(which, at) for which, many in owned for at in range(many)]
        for at, (which, within) in enumerate(found):
            if within == 0:
                for copy in coming[which::count]:
                    copy.wait()
            here = row == block_ref[at if len(owned) > 1 else joined_order[at]]
            for tile in range(tiles):
                weight = jnp.sum(jnp.where(here, tables[tile], 0.0), axis=0, keepdims=True)
                chosen = jnp.sum(
                    jnp.where(here, tables[tiles + tile], 0.0), axis=0, keepdims=True
                )
                into_at = slice(start, start + 128)
                start += 128
                from_at = slice(
                    (within * tiles + tile) * 128, (within * tiles + tile + 1) * 128
                )
                high = chosen.astype(jnp.bfloat16)
                rest = chosen - high.astype(jnp.float32)
                middle = rest.astype(jnp.bfloat16)
                low = rest - middle.astype(jnp.float32)
                split = jnp.where(row == 0, high.astype(jnp.float32), 0.0)
                split = jnp.where(row == 1, middle.astype(jnp.float32), split)
                split = jnp.where(row == 2, low, split)
                split_ref[:, into_at] = split.astype(jnp.bfloat16)
                total = total + hiddens[which][:, from_at].astype(jnp.float32) * weight
                delta_ref[0:hidden, into_at] = (gates[which][:, from_at] * weight).astype(
                    jnp.bfloat16
                )
                delta_ref[hidden : 2 * hidden, into_at] = (
                    ups[which][:, from_at] * weight
                ).astype(jnp.bfloat16)
        base += slots
    spread_ref[...] = jnp.sum(total, axis=1, keepdims=True)


def local_call(kernel, out_shape, *arrays, smem=(), hbm=(), scratch=(), limit=most_vmem):
    vmem = pl.BlockSpec(memory_space=pltpu.VMEM)
    scalar = pl.BlockSpec(memory_space=pltpu.SMEM)
    far = pl.BlockSpec(memory_space=pltpu.HBM)
    return pl.pallas_call(
        kernel,
        out_shape=out_shape,
        in_specs=[
            scalar if at in smem else far if at in hbm else vmem for at in range(len(arrays))
        ],
        out_specs=jax.tree.map(lambda _: vmem, out_shape),
        scratch_shapes=list(scratch),
        compiler_params=pltpu.CompilerParams(vmem_limit_bytes=limit),
        cost_estimate=pl.CostEstimate(flops=1 << 20, bytes_accessed=1 << 21, transcendentals=0),
    )(*arrays)


def shaped(*shape, dtype=jnp.float32):
    return jax.ShapeDtypeStruct(shape, dtype)


def shards(
    tokens,
    norm_gain,
    router_weight,
    value_weight,
    gate_weight,
    up_weight,
    down_weight,
    routes,
    segment_ids,
    loss_mask,
    penalty_reward,
    scores,
):
    tok_count = tokens.shape[1]
    model_width = tokens.shape[2]
    experts = router_weight.shape[0]
    hidden_width = gate_weight.shape[1]
    dp_count = lax.axis_size("dp")
    expert_count = lax.axis_size("expert")
    capacity = tok_count * routes.shape[2] * 3 // (2 * experts)
    own_tokens = tokens[0]
    own_routes = routes[0]
    normed = norm_rows(own_tokens, norm_gain)
    expert_ids = jnp.arange(experts, dtype=jnp.int32)[:, None]
    hit = (own_routes[:, 0][None, :] == expert_ids) | (own_routes[:, 1][None, :] == expert_ids)
    before = jnp.arange(tok_count)[:, None] < jnp.arange(tok_count)[None, :]
    counted = lax.dot_general(
        hit.astype(jnp.bfloat16),
        before.astype(jnp.bfloat16),
        plain,
        preferred_element_type=jnp.float32,
    )
    slot_of = jnp.where(hit, counted, -1.0)
    placed = slot_of[:, None, :] == jnp.arange(capacity, dtype=jnp.float32)[None, :, None]
    down_float = down_weight[0].astype(jnp.float32)
    value_along = jnp.sum(down_float * value_weight[None, :], axis=1, keepdims=True)
    blocks = jnp.stack(relative_blocks(dp_count)).astype(jnp.int32)
    place = lax.axis_index("expert") * dp_count + lax.axis_index("dp")
    place = place.astype(jnp.int32).reshape(1)
    own_stats, opened, reach, shut = local_call(
        first_kernel,
        (shaped(1, 128),) + (shaped(1, tok_count),) * 3,
        segment_ids,
        loss_mask,
        penalty_reward,
        scores,
    )
    rows, turns, made = None, [], []
    all_rows = capacity * expert_count * dp_count
    first = offset = 0
    for turn, share in enumerate(shares):
        slots = capacity * share // sum(shares)
        block_rows = expert_count * slots
        if turn < 2:
            ahead = capacity if turn else slots
            chosen = placed[:, first:ahead].reshape(experts, -1, slots, tok_count)
            chosen = chosen.transpose(1, 0, 2, 3).astype(jnp.bfloat16)
            picked = lax.dot_general(
                chosen.reshape(-1, tok_count),
                normed,
                plain,
                preferred_element_type=jnp.bfloat16,
            ).reshape(-1, experts, slots, model_width)
        sent = picked[max(turn - 1, 0)]
        first += slots
        got = lax.all_to_all(sent, "expert", split_axis=0, concat_axis=0, tiled=True)
        split = turn == len(shares) - 1
        near, far = ring(got.reshape(block_rows, model_width), dp_count, split)
        turns.append((slots, []))
        held = [near, far] if split else [near]
        for pieces in held:
            rows, *results = forward(
                pieces, gate_weight[0], up_weight[0], value_along, rows, offset, all_rows
            )
            many = results[-1].shape[1] // block_rows
            offset += many * block_rows
            turns[-1][1].append((len(made), many))
            made.append(results)
    gates, ups, hiddens, partials = zip(*made)
    width = model_width // dp_count
    own_part = lax.dynamic_slice_in_dim(rows, lax.axis_index("dp") * width, width, axis=1)
    logits = lax.dot_general(
        router_weight, normed.astype(jnp.float32), last_last, precision=highest
    )
    token_value = jnp.sum(own_tokens.astype(jnp.float32) * value_weight[None, :], axis=1)

    outward = local_call(
        functools.partial(pack_kernel, expert_count, turns),
        shaped(expert_count, dp_count, 128),
        blocks,
        *partials,
        own_stats,
        smem=(0,),
    )
    everyone = dp_count * expert_count
    inward = lax.all_to_all(
        outward.reshape(everyone, 128), ("expert", "dp"), 0, 0, tiled=True
    )
    tables, own_values, value_error, loss_part, divisor = local_call(
        functools.partial(value_kernel, capacity),
        (
            shaped(experts, dp_count, 128),
            shaped(1, tok_count),
            shaped(1, tok_count),
            shaped(dp_count, 128),
            shaped(1, 128),
        ),
        place,
        inward.reshape(expert_count, dp_count, 128),
        slot_of,
        logits,
        token_value[None],
        opened,
        reach,
        shut,
        loss_mask,
        smem=(0,),
    )
    owned = lax.all_to_all(
        tables.reshape(everyone, 128), ("expert", "dp"), 0, 0, tiled=True
    )
    token_part = jnp.sum(own_tokens.astype(jnp.float32) * value_error.reshape(tok_count, 1), axis=0)
    delta, spread, split = local_call(
        functools.partial(delta_kernel, capacity, turns),
        (
            shaped(2 * hidden_width, all_rows, dtype=jnp.bfloat16),
            shaped(hidden_width, 1),
            shaped(8, all_rows, dtype=jnp.bfloat16),
        ),
        blocks,
        owned.reshape(expert_count, dp_count, 128),
        *gates,
        *ups,
        *hiddens,
        smem=(0,),
        hbm=range(2, 2 + 3 * len(made)),
        scratch=[pltpu.VMEM(a.shape, a.dtype) for a in gates + ups + hiddens]
        + [pltpu.SemaphoreType.DMA((3 * len(made),))],
        limit=most_vmem,
    )
    tile = model_width // 8
    both_grad = grads(delta, rows, tile, 0, 4, ())
    gate_grad, up_grad = grads(delta, rows, tile, 4, 4, both_grad)
    router_row = lax.dot_general(split, own_part, plain, preferred_element_type=jnp.float32)
    router_row = jnp.sum(router_row, axis=0, keepdims=True)
    down_grad = (spread * value_weight[None, :]).astype(jnp.bfloat16)
    value_part = token_part + jnp.sum(down_float * spread, axis=0)
    parted = jnp.concatenate([value_part.reshape(dp_count, width), loss_part], axis=1)
    parted = lax.all_to_all(parted, "dp", 0, 0, tiled=True)
    parted = jnp.sum(parted, axis=0, keepdims=True)
    last = to_all(jnp.concatenate([parted, router_row], axis=1), "expert")[:, 0]
    value_own = jnp.sum(last[:, : width + 128], axis=0, keepdims=True)
    mean_loss = value_own[0, width] / divisor[0, 0]
    final = to_all(jnp.concatenate([last[:, width + 128 :], value_own[:, :width]], axis=0), "dp")
    router_grad, value_grad = local_call(
        end_kernel, (shaped(experts, model_width), shaped(1, model_width)), final
    )
    return (
        own_values,
        mean_loss,
        value_grad[0],
        router_grad,
        gate_grad[None],
        up_grad[None],
        down_grad[None],
    )


def solution(mesh):
    placed = (
        P("dp", "expert", None),
        P(),
        P(),
        P(),
        P("expert", "dp", None),
        P("expert", "dp", None),
        P("expert", "dp", None),
        P("dp", "expert", None),
        P("dp", "expert"),
        P("dp", "expert"),
        P("dp", "expert"),
        P("dp", None),
    )

    return jax.shard_map(
        shards,
        mesh=mesh,
        in_specs=placed,
        out_specs=(
            P("dp", "expert"),
            P(),
            P(),
            P(),
            P("expert", "dp", None),
            P("expert", "dp", None),
            P("expert", "dp", None),
        ),
        check_vma=False,
    )
```
